32 devices in a mesh: groups: 2 (over y), seq: 8 (over z, x), tensor: 2 (over core).
Axes of the slice: x: 2, y: 2, z: 4, core: 2. Of those that a mesh axis runs over, the one named last changes fastest.
Arguments:
- queries: bfloat16 [4, 1024, 2048], P(('groups', 'tensor'), 'seq'), parts along dimension 0, may hold values from -33 to 33
- keys: bfloat16 [4, 1024, 2048], P(('groups', 'tensor'), 'seq'), parts along dimension 0, may hold values from -33 to 33
- values: bfloat16 [4, 1024, 2048], P(('groups', 'tensor'), 'seq'), parts along dimension 0, may hold values from -6 to 6
- out_grad: bfloat16 [4, 1024, 2048], P(('groups', 'tensor'), 'seq'), parts along dimension 0, may hold values from -96 to 96
- tile_lists: int32 [32, 12], P(('groups', 'tensor')), parts along dimension 0, may hold values from -1 to 15, as said below
Outputs:
- query_grad: bfloat16 [4, 1024, 2048], P(('groups', 'tensor'), 'seq'), parts along dimension 0
- key_grad: bfloat16 [4, 1024, 2048], P(('groups', 'tensor'), 'seq'), parts along dimension 0
- value_grad: bfloat16 [4, 1024, 2048], P(('groups', 'tensor'), 'seq'), parts along dimension 0
The draws below stay inside these ranges and needn't reach their ends.
There are 2 independent parts, one for each index of `groups`. The reference program is written for one: setup_inputs(seed, part) draws one part's arguments, and reference() takes and returns one part's arrays. A program takes and returns all parts, laid end to end along the dimension named above; each array names one. Nothing has to cross between parts.
Inputs may be any that keep to these rules, and one draw needn't show every extreme that they name: `tile_lists`: row i begins with i; its other entries are distinct tiles within 8 of i, followed by -1 entries only where fewer such tiles lie inside the clip.
All inputs are finite; a program needn't handle non-finite values.
Results may differ from the reference program's by a relative error of at most 0.012.
Values may be sent and summed in bfloat16 or wider, within the bound.
A program may use at most 128 MiB of HBM per device.

```python
import math
import jax
import jax.numpy as jnp
from jax import lax

DH = 128
TILE = 128
RADIUS = 8
WIN = 12
HD = 2048
SEGS = 2
SEG = 1024
TILES = 16


def drawn_pair(key):
    key = jax.random.fold_in(key, 11)
    first, second = jax.random.split(key, 2)
    token_count = SEGS * SEG
    base_query = jnp.clip(jax.random.normal(first, (token_count, HD), jnp.float32), -6.0, 6.0)
    base_key = jnp.clip(jax.random.normal(second, (token_count, HD), jnp.float32), -6.0, 6.0)
    key_rows = base_key
    query_rows = base_query
    return (query_rows.reshape(SEGS, SEG, HD), key_rows.reshape(SEGS, SEG, HD))


def draw_queries(key, part):
    return drawn_pair(key)[0].astype(jnp.bfloat16)


def draw_keys(key, part):
    return drawn_pair(key)[1].astype(jnp.bfloat16)


def draw_tile_lists(key, part):
    key = jax.random.fold_in(key, 23)
    offsets = jnp.concatenate([jnp.arange(-RADIUS, 0, dtype=jnp.int32), jnp.arange(1, RADIUS + 1, dtype=jnp.int32)])
    ranking = jax.random.randint(key, (TILES, 2 * RADIUS), 0, 1 << 20, dtype=jnp.int32)
    here = jnp.arange(TILES, dtype=jnp.int32)[:, None]
    target = here + offsets[None, :]
    inside = jnp.logical_and(target >= 0, target < TILES)
    ordering = (1 - inside.astype(jnp.int32)) * (1 << 25) + ranking * 32 + jnp.arange(2 * RADIUS, dtype=jnp.int32)[None, :]
    order = jnp.argsort(ordering, axis=1)[:, :WIN - 1]
    chosen = jnp.take_along_axis(target, order, axis=1)
    chosen_inside = jnp.take_along_axis(inside, order, axis=1)
    chosen = jnp.where(chosen_inside, chosen, -1)
    return jnp.concatenate([here, chosen], 1).astype(jnp.int32)


def block_levels(key, dims, cuts, smallest, top_value):
    def one(dim, blocks):
        heights = jax.random.uniform(jax.random.fold_in(jax.random.fold_in(key, 6), dim), (blocks,), jnp.float32, smallest / len(cuts), top_value / len(cuts))
        return jnp.repeat(jnp.exp(heights), dims[dim] // blocks).reshape((-1,) + (1,) * (len(dims) - dim - 1))

    level = one(*cuts[0])
    for cut in cuts[1:]:
        level = level * one(*cut)
    return level


def centred(stream_key, extent, width, limit, pieces=(), held_as=jnp.bfloat16):
    values = width * jax.random.normal(stream_key, extent, jnp.float32)
    if pieces:
        values = values * block_levels(stream_key, extent, pieces, -0.22, 0.18)
    return jnp.clip(values, -limit, limit).astype(held_as)


def setup_inputs(seed: int = 0, part: int = 0) -> dict:
    seeds = jax.random.split(jax.random.key(seed), 6)
    own_keys = jax.random.split(jax.random.fold_in(seeds[5], part), 6)
    return {
        "queries": draw_queries(jax.random.fold_in(jax.random.fold_in(seeds[5], part), 71), part),
        "keys": draw_keys(jax.random.fold_in(jax.random.fold_in(seeds[5], part), 71), part),
        "values": centred(own_keys[2], (SEGS, SEG, HD), 1.0, 6.0, ((0, 2), (1, 8))),
        "out_grad": centred(own_keys[3], (SEGS, SEG, HD), 16.0, 96.0, ((0, 2), (1, 8))),
        "tile_lists": draw_tile_lists(jax.random.fold_in(jax.random.fold_in(seeds[5], part), 71), part),
    }


def reference(queries, keys, values, out_grad, tile_lists):
    token_count = queries.shape[0] * queries.shape[1]
    feature_count = queries.shape[2]
    head_count = feature_count // DH
    tile_count = token_count // TILE
    score_scale = 1.0 / math.sqrt(DH)

    def per_head(head):

        def head_tiles(array):
            rows = array.reshape(token_count, feature_count)
            return lax.dynamic_slice_in_dim(rows, head * DH, DH, 1).reshape(tile_count, TILE, DH)
        q_tiles = head_tiles(queries)
        k_tiles = head_tiles(keys)
        v_tiles = head_tiles(values)
        g_tiles = head_tiles(out_grad)

        def step(totals, tile_index):
            key_total, value_total = totals
            tile_row = tile_lists[tile_index]
            present = tile_row >= 0
            local_tile = jnp.maximum(tile_row, 0).astype(jnp.int32)
            key_rows = k_tiles[local_tile].reshape(WIN * TILE, DH)
            value_rows = v_tiles[local_tile].reshape(WIN * TILE, DH)
            query_rows = q_tiles[tile_index]
            grad_rows = g_tiles[tile_index]
            scores = jnp.dot(query_rows, key_rows.T, preferred_element_type=jnp.float32) * score_scale
            live_keys = jnp.repeat(present, TILE)
            scores = jnp.where(live_keys[None, :], scores, -1e+30)
            row_max = lax.optimization_barrier(jnp.max(scores, axis=1, keepdims=True))
            weights = jnp.exp(scores - row_max)
            weights = weights / lax.optimization_barrier(jnp.sum(weights, axis=1, keepdims=True))
            weights_b = weights.astype(jnp.bfloat16)
            recomputed = jnp.dot(weights_b, value_rows, preferred_element_type=jnp.float32)
            delta = lax.optimization_barrier(jnp.sum(grad_rows.astype(jnp.float32) * recomputed, axis=1, keepdims=True))
            prob_grad = jnp.dot(grad_rows, value_rows.T, preferred_element_type=jnp.float32)
            score_grad = (weights * (prob_grad - delta) * score_scale).astype(jnp.bfloat16)
            query_part = jnp.dot(score_grad, key_rows, preferred_element_type=jnp.float32).astype(jnp.bfloat16)
            key_part = jnp.dot(score_grad.T, query_rows, preferred_element_type=jnp.float32).reshape(WIN, TILE, DH)
            value_part = jnp.dot(weights_b.T, grad_rows, preferred_element_type=jnp.float32).reshape(WIN, TILE, DH)
            key_total = key_total.at[local_tile].add(key_part)
            value_total = value_total.at[local_tile].add(value_part)
            return ((key_total, value_total), query_part)
        zeros_tiles = jnp.zeros((tile_count, TILE, DH), jnp.float32)
        totals, query_parts = lax.scan(step, (zeros_tiles, zeros_tiles), jnp.arange(tile_count, dtype=jnp.int32))
        key_total, value_total = totals
        return (query_parts.reshape(token_count, DH), key_total.astype(jnp.bfloat16).reshape(token_count, DH), value_total.astype(jnp.bfloat16).reshape(token_count, DH))
    query_heads, key_heads, value_heads = lax.map(per_head, jnp.arange(head_count, dtype=jnp.int32))

    def arrange(array):
        return jnp.transpose(array, (1, 0, 2)).reshape(queries.shape)
    return (arrange(query_heads), arrange(key_heads), arrange(value_heads))
```

```python
import functools
import math

import jax
import jax.numpy as jnp
from jax import lax
from jax.experimental import pallas as pl
from jax.experimental.pallas import tpu as pltpu
from jax.sharding import PartitionSpec as P

HEADS = 16
DH = 128
TILE = 128
RADIUS = 8
WIN = 12


block_tiles = 4


def padded_2(block, sides, width):
    for axis, dim in sides:
        count = lax.axis_size(axis)
        forward = [(i, i + 1) for i in range(count - 1)]
        backward = [(target, source) for source, target in forward]
        low = lax.ppermute(
            lax.slice_in_dim(block, block.shape[dim] - width, None, axis=dim), axis, forward
        )
        high = lax.ppermute(lax.slice_in_dim(block, 0, width, axis=dim), axis, backward)
        block = jnp.concatenate([low, block, high], axis=dim)
    return block


def key_rims(key_rows, value_rows):
    joined = jnp.concatenate([key_rows, value_rows], 1)
    return padded_2(joined, (("tensor", 0),), RADIUS * TILE)


def finish_rims(grads_ext, segment, local_width):
    rim_rows = RADIUS * TILE
    outer_rows = jnp.concatenate([grads_ext[:rim_rows], grads_ext[-rim_rows:]], 0)
    arrived = padded_2(outer_rows, (("tensor", 0),), rim_rows)
    own_rows = grads_ext[rim_rows : rim_rows + segment]
    own_rows = own_rows.at[:rim_rows].add(arrived[:rim_rows])
    own_rows = own_rows.at[segment - rim_rows :].add(arrived[3 * rim_rows :])
    own_rows = own_rows.astype(jnp.bfloat16)
    return (own_rows[:, :local_width], own_rows[:, local_width:])


def regrouped_body(queries, keys, values, out_grad, tile_lists):
    span_rows = queries.shape[1]
    feature_count = queries.shape[2]
    seq_count = lax.axis_size("seq")
    heads_here = HEADS // seq_count
    local_width = heads_here * DH
    score_scale = 1.0 / math.sqrt(DH)
    query_tokens = queries.reshape(span_rows, feature_count)
    key_tokens = keys.reshape(span_rows, feature_count)
    value_tokens = values.reshape(span_rows, feature_count)
    grad_tokens = out_grad.reshape(span_rows, feature_count)
    query_rows, key_rows, value_rows, grad_rows = (
        lax.all_to_all(query_tokens, "seq", split_axis=1, concat_axis=0, tiled=True),
        lax.all_to_all(key_tokens, "seq", split_axis=1, concat_axis=0, tiled=True),
        lax.all_to_all(value_tokens, "seq", split_axis=1, concat_axis=0, tiled=True),
        lax.all_to_all(grad_tokens, "seq", split_axis=1, concat_axis=0, tiled=True),
    )
    padded = key_rims(key_rows, value_rows)
    segment = query_rows.shape[0]
    seg_tiles = segment // TILE
    ext_tiles = seg_tiles + 2 * RADIUS
    block_count = seg_tiles // block_tiles
    first_tile = lax.axis_index("tensor") * seg_tiles - RADIUS
    kv_tiles = padded.reshape(ext_tiles, TILE, 2 * local_width)
    query_blocks = query_rows.reshape(block_count, block_tiles, TILE, heads_here, DH)
    grad_blocks = grad_rows.reshape(block_count, block_tiles, TILE, heads_here, DH)
    list_blocks = tile_lists.reshape(block_count, block_tiles, WIN)

    def attend_block(totals, inputs):
        query_block, grad_block, tile_rows = inputs
        present = tile_rows >= 0
        local_tile = jnp.clip(tile_rows - first_tile, 0, ext_tiles - 1)
        picked = kv_tiles[local_tile].reshape(block_tiles, WIN * TILE, 2, heads_here, DH)
        key_sel = picked[:, :, 0]
        value_sel = picked[:, :, 1]
        scores = (
            jnp.einsum("gthd,gkhd->ghtk", query_block, key_sel, preferred_element_type=jnp.float32)
            * score_scale
        )
        live_keys = jnp.repeat(present, TILE, axis=1)
        scores = jnp.where(live_keys[:, None, None, :], scores, -1e30)
        row_max = jnp.max(scores, axis=3, keepdims=True)
        weights = jnp.exp(scores - row_max)
        weights = weights / jnp.sum(weights, axis=3, keepdims=True)
        weights_b = weights.astype(jnp.bfloat16)
        recomputed = jnp.einsum(
            "ghtk,gkhd->gthd", weights_b, value_sel, preferred_element_type=jnp.float32
        )
        delta = jnp.sum(grad_block.astype(jnp.float32) * recomputed, axis=3)
        prob_grad = jnp.einsum(
            "gthd,gkhd->ghtk", grad_block, value_sel, preferred_element_type=jnp.float32
        )
        score_grad = (
            weights * (prob_grad - jnp.transpose(delta, (0, 2, 1))[..., None]) * score_scale
        ).astype(jnp.bfloat16)
        query_part = jnp.einsum(
            "ghtk,gkhd->gthd", score_grad, key_sel, preferred_element_type=jnp.float32
        ).astype(jnp.bfloat16)
        key_part = jnp.einsum(
            "ghtk,gthd->gkhd", score_grad, query_block, preferred_element_type=jnp.float32
        )
        value_part = jnp.einsum(
            "ghtk,gthd->gkhd", weights_b, grad_block, preferred_element_type=jnp.float32
        )
        key_terms = jnp.concatenate([key_part, value_part], 2).reshape(
            block_tiles, WIN, TILE, 2 * local_width
        )
        totals = totals.at[local_tile].add(key_terms)
        return (totals, query_part)

    initial = jnp.zeros((ext_tiles, TILE, 2 * local_width), jnp.float32)
    grads_ext, query_parts = lax.scan(
        attend_block, initial, (query_blocks, grad_blocks, list_blocks)
    )
    query_grad = query_parts.reshape(segment, local_width)
    grads_ext = grads_ext.reshape(ext_tiles * TILE, 2 * local_width)
    query_back = lax.all_to_all(query_grad, "seq", split_axis=0, concat_axis=1, tiled=True)
    key_grad, value_grad = finish_rims(grads_ext, segment, local_width)
    key_back, value_back = (
        lax.all_to_all(key_grad, "seq", split_axis=0, concat_axis=1, tiled=True),
        lax.all_to_all(value_grad, "seq", split_axis=0, concat_axis=1, tiled=True),
    )
    out_shape = queries.shape
    return (
        query_back.reshape(out_shape),
        key_back.reshape(out_shape),
        value_back.reshape(out_shape),
    )


def partner_order(seq_count, tensor_count):
    order = []
    for step in range(seq_count):
        reach = (seq_count // 2 + ((step + 1) // 2) * (2 * (step % 2) - 1)) % seq_count
        for turn in range(tensor_count):
            if reach or turn:
                order.append((reach, turn))
    return order


def head_kernel(
    seq_count,
    tensor_count,
    q_hbm,
    k_hbm,
    v_hbm,
    g_hbm,
    lists_hbm,
    dq_hbm,
    dk_hbm,
    dv_hbm,
    q_all,
    k_all,
    v_all,
    g_all,
    lists_all,
    bias,
    probs,
    prob_grad,
    key_t,
    dv_sum,
    dk_sum,
    dq_out,
    dk_out,
    dv_out,
    in_send,
    in_recv,
    out_send,
    out_recv,
    list_send,
    list_recv,
    local_sem,
):
    seq_here = lax.axis_index("seq")
    tensor_here = lax.axis_index("tensor")
    me = tensor_here * seq_count + seq_here
    tiles = seq_count * tensor_count
    pairs = tiles // 2
    score_scale = 1.0 / math.sqrt(DH)
    partners = []
    for reach, turn in partner_order(seq_count, tensor_count):
        seq_there = lax.rem(seq_here + reach, seq_count)
        tensor_there = lax.rem(tensor_here + turn, tensor_count)
        partners.append((seq_there, tensor_there, tensor_there * seq_count + seq_there))

    def columns(index):
        return pl.ds(pl.multiple_of(index * DH, DH), DH)

    def remote(src, dst, send, recv, seq_there, tensor_there):
        return pltpu.make_async_remote_copy(
            src_ref=src,
            dst_ref=dst,
            send_sem=send,
            recv_sem=recv,
            device_id={"seq": seq_there, "tensor": tensor_there},
            device_id_type=pl.DeviceIdType.MESH,
        )

    incoming = ((q_hbm, q_all), (k_hbm, k_all), (g_hbm, g_all), (v_hbm, v_all))
    outgoing = ((dv_out, dv_hbm), (dq_out, dq_hbm), (dk_out, dk_hbm))

    def in_copy(which, seq_there, tensor_there, there):
        src, dst = incoming[which]
        return remote(
            src.at[:, columns(there)],
            dst.at[me],
            in_send.at[which, there],
            in_recv.at[which, me],
            seq_there,
            tensor_there,
        )

    def in_wait(which, seq_there, tensor_there, there):
        src, dst = incoming[which]
        remote(
            src.at[:, columns(there)],
            dst.at[there],
            in_send.at[which, there],
            in_recv.at[which, there],
            seq_there,
            tensor_there,
        ).wait()

    def in_local(which):
        src, dst = incoming[which]
        return pltpu.make_async_copy(src.at[:, columns(me)], dst.at[me], local_sem.at[which])

    def out_copy(which, seq_there, tensor_there, there):
        src, dst = outgoing[which]
        return remote(
            src.at[there],
            dst.at[:, columns(me)],
            out_send.at[which, there],
            out_recv.at[which, me],
            seq_there,
            tensor_there,
        )

    def out_wait(which, seq_there, tensor_there, there):
        src, dst = outgoing[which]
        remote(
            src.at[there],
            dst.at[:, columns(there)],
            out_send.at[which, there],
            out_recv.at[which, there],
            seq_there,
            tensor_there,
        ).wait()

    def out_local(which):
        src, dst = outgoing[which]
        return pltpu.make_async_copy(src.at[me], dst.at[:, columns(me)], local_sem.at[4 + which])

    for which in range(4):
        in_local(which).start()
    own_list = pltpu.make_async_copy(lists_hbm, lists_all.at[tensor_here], local_sem.at[7])
    own_list.start()

    barrier = pltpu.get_barrier_semaphore()
    for seq_there, tensor_there, _ in partners:
        pl.semaphore_signal(
            barrier,
            inc=1,
            device_id={"seq": seq_there, "tensor": tensor_there},
            device_id_type=pl.DeviceIdType.MESH,
        )
    pl.semaphore_wait(barrier, len(partners))

    def list_copy(turn, slot):
        return remote(
            lists_hbm,
            lists_all.at[slot],
            list_send.at[turn],
            list_recv.at[slot],
            seq_here,
            lax.rem(tensor_here + turn, tensor_count),
        )

    for turn in range(1, tensor_count):
        list_copy(turn, tensor_here).start()
    for group in ((0, 1), (2,), (3,)):
        for partner in partners:
            for which in group:
                in_copy(which, *partner).start()

    own_list.wait()
    for turn in range(1, tensor_count):
        list_copy(turn, lax.rem(tensor_here + turn, tensor_count)).wait()
    tile_ids = lax.broadcasted_iota(jnp.int32, (tiles, TILE), 0)
    for tile in range(tiles):
        row = lists_all[tile // seq_count, tile % seq_count : tile % seq_count + 1, :]
        miss = jnp.full((tiles, TILE), -1e30, jnp.float32)
        for entry in range(WIN):
            miss = jnp.where(row[:, entry : entry + 1] == tile_ids, 0.0, miss)
        half = (tile % 2) * TILE
        bias[tile // 2, :, half : half + TILE] = miss

    dv_sum[...] = jnp.zeros_like(dv_sum)
    dk_sum[...] = jnp.zeros_like(dk_sum)

    for which in (0, 1):
        in_local(which).wait()
    for partner in partners:
        for which in (0, 1):
            in_wait(which, *partner)

    def pair_rows(ref, index):
        return ref[pl.ds(2 * index, 2)].reshape(2 * TILE, DH)

    def turned(block):
        return block.astype(jnp.float32).T.astype(jnp.bfloat16)

    def key_rows(index):
        return pl.ds(index * 2 * TILE, 2 * TILE)

    def fold(block, op):
        return op(block.reshape(2 * TILE // 8, 8, 2 * TILE), axis=0)

    def score_pair(pair, _):
        query_t = turned(pair_rows(q_all, pair))
        key_t[pair] = turned(pair_rows(k_all, pair))
        top = jnp.full((8, 2 * TILE), -3e38, jnp.float32)
        for chunk in range(pairs):
            scores = (
                jnp.dot(pair_rows(k_all, chunk), query_t, preferred_element_type=jnp.float32)
                * score_scale
            )
            scores = jnp.concatenate(
                [
                    scores[:TILE] + bias[pair, 2 * chunk : 2 * chunk + 1, :],
                    scores[TILE:] + bias[pair, 2 * chunk + 1 : 2 * chunk + 2, :],
                ],
                axis=0,
            )
            probs[pair, key_rows(chunk), :] = scores
            top = jnp.maximum(top, fold(scores, jnp.max))
        top = jnp.max(top, axis=0, keepdims=True)
        total = jnp.zeros((8, 2 * TILE), jnp.float32)
        for chunk in range(pairs):
            weights = jnp.exp(probs[pair, key_rows(chunk), :] - top)
            probs[pair, key_rows(chunk), :] = weights
            total = total + fold(weights, jnp.sum)
        inverse = 1.0 / jnp.sum(total, axis=0, keepdims=True)
        for chunk in range(pairs):
            probs[pair, key_rows(chunk), :] = probs[pair, key_rows(chunk), :] * inverse
        return 0

    lax.fori_loop(0, pairs, score_pair, 0)

    in_local(2).wait()
    for partner in partners:
        in_wait(2, *partner)

    def value_pair(pair, _):
        grad_pair = pair_rows(g_all, pair)
        for chunk in range(pairs):
            dv_sum[key_rows(chunk), :] += jnp.dot(
                probs[pair, key_rows(chunk), :].astype(jnp.bfloat16),
                grad_pair,
                preferred_element_type=jnp.float32,
            )
        return 0

    lax.fori_loop(0, pairs, value_pair, 0)
    dv_out[...] = dv_sum[...].astype(jnp.bfloat16).reshape(dv_out.shape)
    for partner in partners:
        out_copy(0, *partner).start()
    out_local(0).start()

    in_local(3).wait()
    for partner in partners:
        in_wait(3, *partner)

    def grad_pair_step(pair, _):
        query_pair = pair_rows(q_all, pair)
        grad_t = turned(pair_rows(g_all, pair))
        delta = jnp.zeros((8, 2 * TILE), jnp.float32)
        for chunk in range(pairs):
            product = jnp.dot(pair_rows(v_all, chunk), grad_t, preferred_element_type=jnp.float32)
            prob_grad[key_rows(chunk), :] = product
            rounded = probs[pair, key_rows(chunk), :].astype(jnp.bfloat16).astype(jnp.float32)
            delta = delta + fold(rounded * product, jnp.sum)
        delta = jnp.sum(delta, axis=0, keepdims=True)
        query_sum = jnp.zeros((DH, 2 * TILE), jnp.float32)
        for chunk in range(pairs):
            score_grad = (
                probs[pair, key_rows(chunk), :]
                * (prob_grad[key_rows(chunk), :] - delta)
                * score_scale
            ).astype(jnp.bfloat16)
            dk_sum[key_rows(chunk), :] += jnp.dot(
                score_grad, query_pair, preferred_element_type=jnp.float32
            )
            query_sum = query_sum + jnp.dot(
                key_t[chunk], score_grad, preferred_element_type=jnp.float32
            )
        dq_out[pl.ds(2 * pair, 2)] = query_sum.T.astype(jnp.bfloat16).reshape(2, TILE, DH)
        for side in range(2):
            there = 2 * pair + side

            @pl.when(there != me)
            def _():
                out_copy(1, lax.rem(there, seq_count), there // seq_count, there).start()

        return 0

    lax.fori_loop(0, pairs, grad_pair_step, 0)
    dk_out[...] = dk_sum[...].astype(jnp.bfloat16).reshape(dk_out.shape)
    for partner in partners:
        out_copy(2, *partner).start()
    out_local(1).start()
    out_local(2).start()

    for which in range(3):
        out_local(which).wait()
        for partner in partners:
            out_wait(which, *partner)


def head_body(queries, keys, values, out_grad, tile_lists):
    seq_count = lax.axis_size("seq")
    tensor_count = lax.axis_size("tensor")
    tiles = seq_count * tensor_count
    pairs = tiles // 2
    shape = (TILE, HEADS * DH)
    blocks = [array.reshape(shape) for array in (queries, keys, values, out_grad)]
    anywhere = pl.BlockSpec(memory_space=pl.ANY)
    per_tile = pltpu.VMEM((tiles, TILE, DH), jnp.bfloat16)
    grads = pl.pallas_call(
        functools.partial(head_kernel, seq_count, tensor_count),
        out_shape=[jax.ShapeDtypeStruct(shape, jnp.bfloat16)] * 3,
        in_specs=[anywhere] * 5,
        out_specs=[anywhere] * 3,
        scratch_shapes=[
            per_tile,
            per_tile,
            per_tile,
            per_tile,
            pltpu.VMEM((tensor_count,) + tile_lists.shape, jnp.int32),
            pltpu.VMEM((pairs, tiles, 2 * TILE), jnp.float32),
            pltpu.VMEM((pairs, tiles * TILE, 2 * TILE), jnp.float32),
            pltpu.VMEM((tiles * TILE, 2 * TILE), jnp.float32),
            pltpu.VMEM((pairs, DH, 2 * TILE), jnp.bfloat16),
            pltpu.VMEM((tiles * TILE, DH), jnp.float32),
            pltpu.VMEM((tiles * TILE, DH), jnp.float32),
            per_tile,
            per_tile,
            per_tile,
            pltpu.SemaphoreType.DMA((4, tiles)),
            pltpu.SemaphoreType.DMA((4, tiles)),
            pltpu.SemaphoreType.DMA((3, tiles)),
            pltpu.SemaphoreType.DMA((3, tiles)),
            pltpu.SemaphoreType.DMA((tensor_count,)),
            pltpu.SemaphoreType.DMA((tensor_count,)),
            pltpu.SemaphoreType.DMA((8,)),
        ],
        compiler_params=pltpu.CompilerParams(
            collective_id=0, has_side_effects=True, vmem_limit_bytes=60 * 1024 * 1024
        ),
    )(*blocks, tile_lists)
    return tuple(grad.reshape(queries.shape) for grad in grads)


def body(queries, keys, values, out_grad, tile_lists):
    devices = lax.axis_size("seq") * lax.axis_size("tensor")
    one_head_one_tile = devices == HEADS and queries.shape[:2] == (1, TILE)
    if one_head_one_tile and queries.shape[2] == HEADS * DH:
        return head_body(queries, keys, values, out_grad, tile_lists)
    return regrouped_body(queries, keys, values, out_grad, tile_lists)


def solution(mesh):
    return jax.shard_map(
        body,
        mesh=mesh,
        in_specs=(
            P(("groups", "tensor"), "seq", None),
            P(("groups", "tensor"), "seq", None),
            P(("groups", "tensor"), "seq", None),
            P(("groups", "tensor"), "seq", None),
            P(("groups", "tensor"), None),
        ),
        out_specs=(
            P(("groups", "tensor"), "seq", None),
            P(("groups", "tensor"), "seq", None),
            P(("groups", "tensor"), "seq", None),
        ),
        check_vma=False,
    )
```

```python
import functools
import math

import jax
import jax.numpy as jnp
from jax import lax
from jax.experimental import pallas as pl
from jax.experimental.pallas import tpu as pltpu
from jax.sharding import PartitionSpec as P

HEADS = 16
DH = 128
TILE = 128
RADIUS = 8
WIN = 12


block_tiles = 4


def padded_2(block, sides, width):
    for axis, dim in sides:
        count = lax.axis_size(axis)
        forward = [(i, i + 1) for i in range(count - 1)]
        backward = [(target, source) for source, target in forward]
        low = lax.ppermute(
            lax.slice_in_dim(block, block.shape[dim] - width, None, axis=dim), axis, forward
        )
        high = lax.ppermute(lax.slice_in_dim(block, 0, width, axis=dim), axis, backward)
        block = jnp.concatenate([low, block, high], axis=dim)
    return block


def key_rims(key_rows, value_rows):
    joined = jnp.concatenate([key_rows, value_rows], 1)
    return padded_2(joined, (("tensor", 0),), RADIUS * TILE)


def finish_rims(grads_ext, segment, local_width):
    rim_rows = RADIUS * TILE
    outer_rows = jnp.concatenate([grads_ext[:rim_rows], grads_ext[-rim_rows:]], 0)
    arrived = padded_2(outer_rows, (("tensor", 0),), rim_rows)
    own_rows = grads_ext[rim_rows : rim_rows + segment]
    own_rows = own_rows.at[:rim_rows].add(arrived[:rim_rows])
    own_rows = own_rows.at[segment - rim_rows :].add(arrived[3 * rim_rows :])
    own_rows = own_rows.astype(jnp.bfloat16)
    return (own_rows[:, :local_width], own_rows[:, local_width:])


def regrouped_body(queries, keys, values, out_grad, tile_lists):
    span_rows = queries.shape[1]
    feature_count = queries.shape[2]
    seq_count = lax.axis_size("seq")
    heads_here = HEADS // seq_count
    local_width = heads_here * DH
    score_scale = 1.0 / math.sqrt(DH)
    query_tokens = queries.reshape(span_rows, feature_count)
    key_tokens = keys.reshape(span_rows, feature_count)
    value_tokens = values.reshape(span_rows, feature_count)
    grad_tokens = out_grad.reshape(span_rows, feature_count)
    query_rows, key_rows, value_rows, grad_rows = (
        lax.all_to_all(query_tokens, "seq", split_axis=1, concat_axis=0, tiled=True),
        lax.all_to_all(key_tokens, "seq", split_axis=1, concat_axis=0, tiled=True),
        lax.all_to_all(value_tokens, "seq", split_axis=1, concat_axis=0, tiled=True),
        lax.all_to_all(grad_tokens, "seq", split_axis=1, concat_axis=0, tiled=True),
    )
    padded = key_rims(key_rows, value_rows)
    segment = query_rows.shape[0]
    seg_tiles = segment // TILE
    ext_tiles = seg_tiles + 2 * RADIUS
    block_count = seg_tiles // block_tiles
    first_tile = lax.axis_index("tensor") * seg_tiles - RADIUS
    kv_tiles = padded.reshape(ext_tiles, TILE, 2 * local_width)
    query_blocks = query_rows.reshape(block_count, block_tiles, TILE, heads_here, DH)
    grad_blocks = grad_rows.reshape(block_count, block_tiles, TILE, heads_here, DH)
    list_blocks = tile_lists.reshape(block_count, block_tiles, WIN)

    def attend_block(totals, inputs):
        query_block, grad_block, tile_rows = inputs
        present = tile_rows >= 0
        local_tile = jnp.clip(tile_rows - first_tile, 0, ext_tiles - 1)
        picked = kv_tiles[local_tile].reshape(block_tiles, WIN * TILE, 2, heads_here, DH)
        key_sel = picked[:, :, 0]
        value_sel = picked[:, :, 1]
        scores = (
            jnp.einsum("gthd,gkhd->ghtk", query_block, key_sel, preferred_element_type=jnp.float32)
            * score_scale
        )
        live_keys = jnp.repeat(present, TILE, axis=1)
        scores = jnp.where(live_keys[:, None, None, :], scores, -1e30)
        row_max = jnp.max(scores, axis=3, keepdims=True)
        weights = jnp.exp(scores - row_max)
        weights = weights / jnp.sum(weights, axis=3, keepdims=True)
        weights_b = weights.astype(jnp.bfloat16)
        recomputed = jnp.einsum(
            "ghtk,gkhd->gthd", weights_b, value_sel, preferred_element_type=jnp.float32
        )
        delta = jnp.sum(grad_block.astype(jnp.float32) * recomputed, axis=3)
        prob_grad = jnp.einsum(
            "gthd,gkhd->ghtk", grad_block, value_sel, preferred_element_type=jnp.float32
        )
        score_grad = (
            weights * (prob_grad - jnp.transpose(delta, (0, 2, 1))[..., None]) * score_scale
        ).astype(jnp.bfloat16)
        query_part = jnp.einsum(
            "ghtk,gkhd->gthd", score_grad, key_sel, preferred_element_type=jnp.float32
        ).astype(jnp.bfloat16)
        key_part = jnp.einsum(
            "ghtk,gthd->gkhd", score_grad, query_block, preferred_element_type=jnp.float32
        )
        value_part = jnp.einsum(
            "ghtk,gthd->gkhd", weights_b, grad_block, preferred_element_type=jnp.float32
        )
        key_terms = jnp.concatenate([key_part, value_part], 2).reshape(
            block_tiles, WIN, TILE, 2 * local_width
        )
        totals = totals.at[local_tile].add(key_terms)
        return (totals, query_part)

    initial = jnp.zeros((ext_tiles, TILE, 2 * local_width), jnp.float32)
    grads_ext, query_parts = lax.scan(
        attend_block, initial, (query_blocks, grad_blocks, list_blocks)
    )
    query_grad = query_parts.reshape(segment, local_width)
    grads_ext = grads_ext.reshape(ext_tiles * TILE, 2 * local_width)
    query_back = lax.all_to_all(query_grad, "seq", split_axis=0, concat_axis=1, tiled=True)
    key_grad, value_grad = finish_rims(grads_ext, segment, local_width)
    key_back, value_back = (
        lax.all_to_all(key_grad, "seq", split_axis=0, concat_axis=1, tiled=True),
        lax.all_to_all(value_grad, "seq", split_axis=0, concat_axis=1, tiled=True),
    )
    out_shape = queries.shape
    return (
        query_back.reshape(out_shape),
        key_back.reshape(out_shape),
        value_back.reshape(out_shape),
    )


def partner_order(seq_count, tensor_count):
    order = []
    for step in range(seq_count):
        reach = (seq_count // 2 + ((step + 1) // 2) * (2 * (step % 2) - 1)) % seq_count
        for turn in range(tensor_count):
            if reach or turn:
                order.append((reach, turn))
    return order


def head_kernel(
    seq_count,
    tensor_count,
    q_hbm,
    k_hbm,
    v_hbm,
    g_hbm,
    lists_hbm,
    dq_hbm,
    dk_hbm,
    dv_hbm,
    q_all,
    k_all,
    v_all,
    g_all,
    lists_all,
    bias,
    probs,
    prob_grad,
    key_t,
    dv_sum,
    dk_sum,
    dq_out,
    dk_out,
    dv_out,
    staged,
    in_send,
    in_recv,
    out_send,
    out_recv,
    list_send,
    list_recv,
    local_sem,
):
    seq_here = lax.axis_index("seq")
    tensor_here = lax.axis_index("tensor")
    me = tensor_here * seq_count + seq_here
    tiles = seq_count * tensor_count
    pairs = tiles // 2
    score_scale = 1.0 / math.sqrt(DH)
    partners = []
    for reach, turn in partner_order(seq_count, tensor_count):
        seq_there = lax.rem(seq_here + reach, seq_count)
        tensor_there = lax.rem(tensor_here + turn, tensor_count)
        partners.append((seq_there, tensor_there, tensor_there * seq_count + seq_there))

    def columns(index):
        return pl.ds(pl.multiple_of(index * DH, DH), DH)

    def remote(src, dst, send, recv, seq_there, tensor_there):
        return pltpu.make_async_remote_copy(
            src_ref=src,
            dst_ref=dst,
            send_sem=send,
            recv_sem=recv,
            device_id={"seq": seq_there, "tensor": tensor_there},
            device_id_type=pl.DeviceIdType.MESH,
        )

    staging = [
        pltpu.make_async_copy(src, staged.at[which], local_sem.at[8 + which])
        for which, src in enumerate((q_hbm, k_hbm, g_hbm, v_hbm))
    ]
    incoming = tuple(
        (staged.at[which], dst) for which, dst in enumerate((q_all, k_all, g_all, v_all))
    )
    outgoing = ((dv_out, dv_hbm), (dq_out, dq_hbm), (dk_out, dk_hbm))

    def in_copy(which, seq_there, tensor_there, there):
        src, dst = incoming[which]
        return remote(
            src.at[:, columns(there)],
            dst.at[me],
            in_send.at[which, there],
            in_recv.at[which, me],
            seq_there,
            tensor_there,
        )

    def in_wait(which, seq_there, tensor_there, there):
        src, dst = incoming[which]
        remote(
            src.at[:, columns(there)],
            dst.at[there],
            in_send.at[which, there],
            in_recv.at[which, there],
            seq_there,
            tensor_there,
        ).wait()

    def in_local(which):
        src, dst = incoming[which]
        return pltpu.make_async_copy(src.at[:, columns(me)], dst.at[me], local_sem.at[which])

    def out_copy(which, seq_there, tensor_there, there):
        src, dst = outgoing[which]
        return remote(
            src.at[there],
            dst.at[:, columns(me)],
            out_send.at[which, there],
            out_recv.at[which, me],
            seq_there,
            tensor_there,
        )

    def out_wait(which, seq_there, tensor_there, there):
        src, dst = outgoing[which]
        remote(
            src.at[there],
            dst.at[:, columns(there)],
            out_send.at[which, there],
            out_recv.at[which, there],
            seq_there,
            tensor_there,
        ).wait()

    def out_local(which):
        src, dst = outgoing[which]
        return pltpu.make_async_copy(src.at[me], dst.at[:, columns(me)], local_sem.at[4 + which])

    for copy in staging:
        copy.start()
    own_list = pltpu.make_async_copy(lists_hbm, lists_all.at[tensor_here], local_sem.at[7])
    own_list.start()

    barrier = pltpu.get_barrier_semaphore()
    for seq_there, tensor_there, _ in partners:
        pl.semaphore_signal(
            barrier,
            inc=1,
            device_id={"seq": seq_there, "tensor": tensor_there},
            device_id_type=pl.DeviceIdType.MESH,
        )
    pl.semaphore_wait(barrier, len(partners))

    def list_copy(turn, slot):
        return remote(
            lists_hbm,
            lists_all.at[slot],
            list_send.at[turn],
            list_recv.at[slot],
            seq_here,
            lax.rem(tensor_here + turn, tensor_count),
        )

    for turn in range(1, tensor_count):
        list_copy(turn, tensor_here).start()
    for group in ((0, 1), (2,), (3,)):
        for which in group:
            staging[which].wait()
            in_local(which).start()
        for partner in partners:
            for which in group:
                in_copy(which, *partner).start()

    own_list.wait()
    for turn in range(1, tensor_count):
        list_copy(turn, lax.rem(tensor_here + turn, tensor_count)).wait()
    tile_ids = lax.broadcasted_iota(jnp.int32, (tiles, TILE), 0)
    for tile in range(tiles):
        row = lists_all[tile // seq_count, tile % seq_count : tile % seq_count + 1, :]
        miss = jnp.full((tiles, TILE), -1e30, jnp.float32)
        for entry in range(WIN):
            miss = jnp.where(row[:, entry : entry + 1] == tile_ids, 0.0, miss)
        half = (tile % 2) * TILE
        bias[tile // 2, :, half : half + TILE] = miss

    dv_sum[...] = jnp.zeros_like(dv_sum)
    dk_sum[...] = jnp.zeros_like(dk_sum)

    for which in (0, 1):
        in_local(which).wait()
    for partner in partners:
        for which in (0, 1):
            in_wait(which, *partner)

    def pair_rows(ref, index):
        return ref[pl.ds(2 * index, 2)].reshape(2 * TILE, DH)

    def turned(block):
        return block.astype(jnp.float32).T.astype(jnp.bfloat16)

    def key_rows(index):
        return pl.ds(index * 2 * TILE, 2 * TILE)

    def fold(block, op):
        return op(block.reshape(2 * TILE // 8, 8, 2 * TILE), axis=0)

    def score_pair(pair, _):
        query_t = turned(pair_rows(q_all, pair))
        key_t[pair] = turned(pair_rows(k_all, pair))
        top = jnp.full((8, 2 * TILE), -3e38, jnp.float32)
        for chunk in range(pairs):
            scores = (
                jnp.dot(pair_rows(k_all, chunk), query_t, preferred_element_type=jnp.float32)
                * score_scale
            )
            scores = jnp.concatenate(
                [
                    scores[:TILE] + bias[pair, 2 * chunk : 2 * chunk + 1, :],
                    scores[TILE:] + bias[pair, 2 * chunk + 1 : 2 * chunk + 2, :],
                ],
                axis=0,
            )
            probs[pair, key_rows(chunk), :] = scores
            top = jnp.maximum(top, fold(scores, jnp.max))
        top = jnp.max(top, axis=0, keepdims=True)
        total = jnp.zeros((8, 2 * TILE), jnp.float32)
        for chunk in range(pairs):
            weights = jnp.exp(probs[pair, key_rows(chunk), :] - top)
            probs[pair, key_rows(chunk), :] = weights
            total = total + fold(weights, jnp.sum)
        inverse = 1.0 / jnp.sum(total, axis=0, keepdims=True)
        for chunk in range(pairs):
            probs[pair, key_rows(chunk), :] = probs[pair, key_rows(chunk), :] * inverse
        return 0

    lax.fori_loop(0, pairs, score_pair, 0)

    in_local(2).wait()
    for partner in partners:
        in_wait(2, *partner)

    def value_pair(pair, _):
        grad_pair = pair_rows(g_all, pair)
        for chunk in range(pairs):
            dv_sum[key_rows(chunk), :] += jnp.dot(
                probs[pair, key_rows(chunk), :].astype(jnp.bfloat16),
                grad_pair,
                preferred_element_type=jnp.float32,
            )
        return 0

    lax.fori_loop(0, pairs, value_pair, 0)
    dv_out[...] = dv_sum[...].astype(jnp.bfloat16).reshape(dv_out.shape)
    for partner in partners:
        out_copy(0, *partner).start()
    out_local(0).start()

    in_local(3).wait()
    for partner in partners:
        in_wait(3, *partner)

    def grad_pair_step(pair, _):
        query_pair = pair_rows(q_all, pair)
        grad_t = turned(pair_rows(g_all, pair))
        delta = jnp.zeros((8, 2 * TILE), jnp.float32)
        for chunk in range(pairs):
            product = jnp.dot(pair_rows(v_all, chunk), grad_t, preferred_element_type=jnp.float32)
            prob_grad[key_rows(chunk), :] = product
            rounded = probs[pair, key_rows(chunk), :].astype(jnp.bfloat16).astype(jnp.float32)
            delta = delta + fold(rounded * product, jnp.sum)
        delta = jnp.sum(delta, axis=0, keepdims=True)
        query_sum = jnp.zeros((DH, 2 * TILE), jnp.float32)
        for chunk in range(pairs):
            score_grad = (
                probs[pair, key_rows(chunk), :]
                * (prob_grad[key_rows(chunk), :] - delta)
                * score_scale
            ).astype(jnp.bfloat16)
            dk_sum[key_rows(chunk), :] += jnp.dot(
                score_grad, query_pair, preferred_element_type=jnp.float32
            )
            query_sum = query_sum + jnp.dot(
                key_t[chunk], score_grad, preferred_element_type=jnp.float32
            )
        dq_out[pl.ds(2 * pair, 2)] = query_sum.T.astype(jnp.bfloat16).reshape(2, TILE, DH)
        for side in range(2):
            there = 2 * pair + side

            @pl.when(there != me)
            def _():
                out_copy(1, lax.rem(there, seq_count), there // seq_count, there).start()

        return 0

    lax.fori_loop(0, pairs, grad_pair_step, 0)
    dk_out[...] = dk_sum[...].astype(jnp.bfloat16).reshape(dk_out.shape)
    for partner in partners:
        out_copy(2, *partner).start()
    out_local(1).start()
    out_local(2).start()

    for which in range(3):
        out_local(which).wait()
        for partner in partners:
            out_wait(which, *partner)


def settle_kernel(*refs):
    copies = [
        pltpu.make_async_copy(src, dst, refs[6].at[i])
        for i, (src, dst) in enumerate(zip(refs[:3], refs[3:6]))
    ]
    for copy in copies:
        copy.start()
    for copy in copies:
        copy.wait()


def settle(grads):
    anywhere = pl.BlockSpec(memory_space=pl.ANY)
    return pl.pallas_call(
        settle_kernel,
        out_shape=[pltpu.HBM(grad.shape, grad.dtype) for grad in grads],
        in_specs=[anywhere] * 3,
        out_specs=[anywhere] * 3,
        scratch_shapes=[pltpu.SemaphoreType.DMA((3,))],
    )(*[pltpu.with_memory_space_constraint(grad, pltpu.VMEM) for grad in grads])


def head_body(queries, keys, values, out_grad, tile_lists):
    seq_count = lax.axis_size("seq")
    tensor_count = lax.axis_size("tensor")
    tiles = seq_count * tensor_count
    pairs = tiles // 2
    shape = (TILE, HEADS * DH)
    blocks = [array.reshape(shape) for array in (queries, keys, values, out_grad)]
    anywhere = pl.BlockSpec(memory_space=pl.ANY)
    per_tile = pltpu.VMEM((tiles, TILE, DH), jnp.bfloat16)
    grads = pl.pallas_call(
        functools.partial(head_kernel, seq_count, tensor_count),
        out_shape=[pltpu.VMEM(shape, jnp.bfloat16)] * 3,
        in_specs=[anywhere] * 5,
        out_specs=[anywhere] * 3,
        scratch_shapes=[
            per_tile,
            per_tile,
            per_tile,
            per_tile,
            pltpu.VMEM((tensor_count,) + tile_lists.shape, jnp.int32),
            pltpu.VMEM((pairs, tiles, 2 * TILE), jnp.float32),
            pltpu.VMEM((pairs, tiles * TILE, 2 * TILE), jnp.float32),
            pltpu.VMEM((tiles * TILE, 2 * TILE), jnp.float32),
            pltpu.VMEM((pairs, DH, 2 * TILE), jnp.bfloat16),
            pltpu.VMEM((tiles * TILE, DH), jnp.float32),
            pltpu.VMEM((tiles * TILE, DH), jnp.float32),
            per_tile,
            per_tile,
            per_tile,
            pltpu.VMEM((4,) + shape, jnp.bfloat16),
            pltpu.SemaphoreType.DMA((4, tiles)),
            pltpu.SemaphoreType.DMA((4, tiles)),
            pltpu.SemaphoreType.DMA((3, tiles)),
            pltpu.SemaphoreType.DMA((3, tiles)),
            pltpu.SemaphoreType.DMA((tensor_count,)),
            pltpu.SemaphoreType.DMA((tensor_count,)),
            pltpu.SemaphoreType.DMA((12,)),
        ],
        compiler_params=pltpu.CompilerParams(
            collective_id=0, has_side_effects=True, vmem_limit_bytes=60 * 1024 * 1024
        ),
    )(*blocks, tile_lists)
    return tuple(grad.reshape(queries.shape) for grad in settle(grads))


def body(queries, keys, values, out_grad, tile_lists):
    devices = lax.axis_size("seq") * lax.axis_size("tensor")
    one_head_one_tile = devices == HEADS and queries.shape[:2] == (1, TILE)
    if one_head_one_tile and queries.shape[2] == HEADS * DH:
        return head_body(queries, keys, values, out_grad, tile_lists)
    return regrouped_body(queries, keys, values, out_grad, tile_lists)


def solution(mesh):
    return jax.shard_map(
        body,
        mesh=mesh,
        in_specs=(
            P(("groups", "tensor"), "seq", None),
            P(("groups", "tensor"), "seq", None),
            P(("groups", "tensor"), "seq", None),
            P(("groups", "tensor"), "seq", None),
            P(("groups", "tensor"), None),
        ),
        out_specs=(
            P(("groups", "tensor"), "seq", None),
            P(("groups", "tensor"), "seq", None),
            P(("groups", "tensor"), "seq", None),
        ),
        check_vma=False,
    )
```

```python
import functools
import math

import jax
import jax.numpy as jnp
from jax import lax
from jax.experimental import pallas as pl
from jax.experimental.pallas import tpu as pltpu
from jax.sharding import PartitionSpec as P

HEADS = 16
DH = 128
TILE = 128
RADIUS = 8
WIN = 12


block_tiles = 4


def padded_2(block, sides, width):
    for axis, dim in sides:
        count = lax.axis_size(axis)
        forward = [(i, i + 1) for i in range(count - 1)]
        backward = [(target, source) for source, target in forward]
        low = lax.ppermute(
            lax.slice_in_dim(block, block.shape[dim] - width, None, axis=dim), axis, forward
        )
        high = lax.ppermute(lax.slice_in_dim(block, 0, width, axis=dim), axis, backward)
        block = jnp.concatenate([low, block, high], axis=dim)
    return block


def key_rims(key_rows, value_rows):
    joined = jnp.concatenate([key_rows, value_rows], 1)
    return padded_2(joined, (("tensor", 0),), RADIUS * TILE)


def finish_rims(grads_ext, segment, local_width):
    rim_rows = RADIUS * TILE
    outer_rows = jnp.concatenate([grads_ext[:rim_rows], grads_ext[-rim_rows:]], 0)
    arrived = padded_2(outer_rows, (("tensor", 0),), rim_rows)
    own_rows = grads_ext[rim_rows : rim_rows + segment]
    own_rows = own_rows.at[:rim_rows].add(arrived[:rim_rows])
    own_rows = own_rows.at[segment - rim_rows :].add(arrived[3 * rim_rows :])
    own_rows = own_rows.astype(jnp.bfloat16)
    return (own_rows[:, :local_width], own_rows[:, local_width:])


def regrouped_body(queries, keys, values, out_grad, tile_lists):
    span_rows = queries.shape[1]
    feature_count = queries.shape[2]
    seq_count = lax.axis_size("seq")
    heads_here = HEADS // seq_count
    local_width = heads_here * DH
    score_scale = 1.0 / math.sqrt(DH)
    query_tokens = queries.reshape(span_rows, feature_count)
    key_tokens = keys.reshape(span_rows, feature_count)
    value_tokens = values.reshape(span_rows, feature_count)
    grad_tokens = out_grad.reshape(span_rows, feature_count)
    query_rows, key_rows, value_rows, grad_rows = (
        lax.all_to_all(query_tokens, "seq", split_axis=1, concat_axis=0, tiled=True),
        lax.all_to_all(key_tokens, "seq", split_axis=1, concat_axis=0, tiled=True),
        lax.all_to_all(value_tokens, "seq", split_axis=1, concat_axis=0, tiled=True),
        lax.all_to_all(grad_tokens, "seq", split_axis=1, concat_axis=0, tiled=True),
    )
    padded = key_rims(key_rows, value_rows)
    segment = query_rows.shape[0]
    seg_tiles = segment // TILE
    ext_tiles = seg_tiles + 2 * RADIUS
    block_count = seg_tiles // block_tiles
    first_tile = lax.axis_index("tensor") * seg_tiles - RADIUS
    kv_tiles = padded.reshape(ext_tiles, TILE, 2 * local_width)
    query_blocks = query_rows.reshape(block_count, block_tiles, TILE, heads_here, DH)
    grad_blocks = grad_rows.reshape(block_count, block_tiles, TILE, heads_here, DH)
    list_blocks = tile_lists.reshape(block_count, block_tiles, WIN)

    def attend_block(totals, inputs):
        query_block, grad_block, tile_rows = inputs
        present = tile_rows >= 0
        local_tile = jnp.clip(tile_rows - first_tile, 0, ext_tiles - 1)
        picked = kv_tiles[local_tile].reshape(block_tiles, WIN * TILE, 2, heads_here, DH)
        key_sel = picked[:, :, 0]
        value_sel = picked[:, :, 1]
        scores = (
            jnp.einsum("gthd,gkhd->ghtk", query_block, key_sel, preferred_element_type=jnp.float32)
            * score_scale
        )
        live_keys = jnp.repeat(present, TILE, axis=1)
        scores = jnp.where(live_keys[:, None, None, :], scores, -1e30)
        row_max = jnp.max(scores, axis=3, keepdims=True)
        weights = jnp.exp(scores - row_max)
        weights = weights / jnp.sum(weights, axis=3, keepdims=True)
        weights_b = weights.astype(jnp.bfloat16)
        recomputed = jnp.einsum(
            "ghtk,gkhd->gthd", weights_b, value_sel, preferred_element_type=jnp.float32
        )
        delta = jnp.sum(grad_block.astype(jnp.float32) * recomputed, axis=3)
        prob_grad = jnp.einsum(
            "gthd,gkhd->ghtk", grad_block, value_sel, preferred_element_type=jnp.float32
        )
        score_grad = (
            weights * (prob_grad - jnp.transpose(delta, (0, 2, 1))[..., None]) * score_scale
        ).astype(jnp.bfloat16)
        query_part = jnp.einsum(
            "ghtk,gkhd->gthd", score_grad, key_sel, preferred_element_type=jnp.float32
        ).astype(jnp.bfloat16)
        key_part = jnp.einsum(
            "ghtk,gthd->gkhd", score_grad, query_block, preferred_element_type=jnp.float32
        )
        value_part = jnp.einsum(
            "ghtk,gthd->gkhd", weights_b, grad_block, preferred_element_type=jnp.float32
        )
        key_terms = jnp.concatenate([key_part, value_part], 2).reshape(
            block_tiles, WIN, TILE, 2 * local_width
        )
        totals = totals.at[local_tile].add(key_terms)
        return (totals, query_part)

    initial = jnp.zeros((ext_tiles, TILE, 2 * local_width), jnp.float32)
    grads_ext, query_parts = lax.scan(
        attend_block, initial, (query_blocks, grad_blocks, list_blocks)
    )
    query_grad = query_parts.reshape(segment, local_width)
    grads_ext = grads_ext.reshape(ext_tiles * TILE, 2 * local_width)
    query_back = lax.all_to_all(query_grad, "seq", split_axis=0, concat_axis=1, tiled=True)
    key_grad, value_grad = finish_rims(grads_ext, segment, local_width)
    key_back, value_back = (
        lax.all_to_all(key_grad, "seq", split_axis=0, concat_axis=1, tiled=True),
        lax.all_to_all(value_grad, "seq", split_axis=0, concat_axis=1, tiled=True),
    )
    out_shape = queries.shape
    return (
        query_back.reshape(out_shape),
        key_back.reshape(out_shape),
        value_back.reshape(out_shape),
    )


def partner_order(seq_count, tensor_count):
    order = []
    for step in range(seq_count):
        reach = (seq_count // 2 + ((step + 1) // 2) * (1 - 2 * (step % 2))) % seq_count
        for turn in range(tensor_count):
            if reach or turn:
                order.append((reach, turn))
    return order


def head_kernel(
    seq_count,
    tensor_count,
    q_hbm,
    k_hbm,
    v_hbm,
    g_hbm,
    lists_hbm,
    dq_hbm,
    dk_hbm,
    dv_hbm,
    qk_all,
    v_all,
    g_all,
    lists_all,
    bias,
    probs,
    prob_grad,
    key_t,
    dv_sum,
    dk_sum,
    dq_out,
    dk_out,
    dv_out,
    staged,
    in_send,
    in_recv,
    out_send,
    out_recv,
    list_send,
    list_recv,
    local_sem,
):
    seq_here = lax.axis_index("seq")
    tensor_here = lax.axis_index("tensor")
    me = tensor_here * seq_count + seq_here
    tiles = seq_count * tensor_count
    pairs = tiles // 2
    score_scale = 1.0 / math.sqrt(DH)
    partners = []
    for reach, turn in partner_order(seq_count, tensor_count):
        seq_there = lax.rem(seq_here + reach, seq_count)
        tensor_there = lax.rem(tensor_here + turn, tensor_count)
        partners.append((seq_there, tensor_there, tensor_there * seq_count + seq_there))

    def columns(index):
        return pl.ds(pl.multiple_of(index * DH, DH), DH)

    def remote(src, dst, send, recv, seq_there, tensor_there):
        return pltpu.make_async_remote_copy(
            src_ref=src,
            dst_ref=dst,
            send_sem=send,
            recv_sem=recv,
            device_id={"seq": seq_there, "tensor": tensor_there},
            device_id_type=pl.DeviceIdType.MESH,
        )

    staging = [
        pltpu.make_async_copy(src, staged.at[which], local_sem.at[8 + which])
        for which, src in enumerate((q_hbm, k_hbm, g_hbm, v_hbm))
    ]
    q_all, k_all = qk_all.at[0], qk_all.at[1]
    incoming = {
        0: (lambda cols: staged.at[pl.ds(0, 2), :, cols], lambda slot: qk_all.at[:, slot]),
        2: (lambda cols: staged.at[2, :, cols], lambda slot: g_all.at[slot]),
        3: (lambda cols: staged.at[3, :, cols], lambda slot: v_all.at[slot]),
    }
    outgoing = ((dv_out, dv_hbm), (dq_out, dq_hbm), (dk_out, dk_hbm))

    def in_copy(which, seq_there, tensor_there, there):
        src, dst = incoming[which]
        return remote(
            src(columns(there)),
            dst(me),
            in_send.at[which, there],
            in_recv.at[which, me],
            seq_there,
            tensor_there,
        )

    def in_wait(which, seq_there, tensor_there, there):
        src, dst = incoming[which]
        remote(
            src(columns(there)),
            dst(there),
            in_send.at[which, there],
            in_recv.at[which, there],
            seq_there,
            tensor_there,
        ).wait()

    def in_local(which):
        src, dst = incoming[which]
        return pltpu.make_async_copy(src(columns(me)), dst(me), local_sem.at[which])

    def out_copy(which, seq_there, tensor_there, there):
        src, dst = outgoing[which]
        return remote(
            src.at[there],
            dst.at[:, columns(me)],
            out_send.at[which, there],
            out_recv.at[which, me],
            seq_there,
            tensor_there,
        )

    def out_wait(which, seq_there, tensor_there, there):
        src, dst = outgoing[which]
        remote(
            src.at[there],
            dst.at[:, columns(there)],
            out_send.at[which, there],
            out_recv.at[which, there],
            seq_there,
            tensor_there,
        ).wait()

    def out_local(which):
        src, dst = outgoing[which]
        return pltpu.make_async_copy(src.at[me], dst.at[:, columns(me)], local_sem.at[4 + which])

    for copy in staging:
        copy.start()
    own_list = pltpu.make_async_copy(lists_hbm, lists_all.at[tensor_here], local_sem.at[7])
    own_list.start()

    barrier = pltpu.get_barrier_semaphore()
    for seq_there, tensor_there, _ in partners:
        pl.semaphore_signal(
            barrier,
            inc=1,
            device_id={"seq": seq_there, "tensor": tensor_there},
            device_id_type=pl.DeviceIdType.MESH,
        )
    pl.semaphore_wait(barrier, len(partners))

    def list_copy(turn, slot):
        return remote(
            lists_hbm,
            lists_all.at[slot],
            list_send.at[turn],
            list_recv.at[slot],
            seq_here,
            lax.rem(tensor_here + turn, tensor_count),
        )

    for turn in range(1, tensor_count):
        list_copy(turn, tensor_here).start()
    for group in ((0, 1), (2,), (3,)):
        for which in group:
            staging[which].wait()
        in_local(group[0]).start()
        for partner in partners:
            in_copy(group[0], *partner).start()

    own_list.wait()
    for turn in range(1, tensor_count):
        list_copy(turn, lax.rem(tensor_here + turn, tensor_count)).wait()
    tile_ids = lax.broadcasted_iota(jnp.int32, (tiles, TILE), 0)
    for tile in range(tiles):
        row = lists_all[tile // seq_count, tile % seq_count : tile % seq_count + 1, :]
        miss = jnp.full((tiles, TILE), -1e30, jnp.float32)
        for entry in range(WIN):
            miss = jnp.where(row[:, entry : entry + 1] == tile_ids, 0.0, miss)
        half = (tile % 2) * TILE
        bias[tile // 2, :, half : half + TILE] = miss

    dv_sum[...] = jnp.zeros_like(dv_sum)
    dk_sum[...] = jnp.zeros_like(dk_sum)

    in_local(0).wait()
    for partner in partners:
        in_wait(0, *partner)

    def pair_rows(ref, index):
        return ref[pl.ds(2 * index, 2)].reshape(2 * TILE, DH)

    def turned(block):
        return block.astype(jnp.float32).T.astype(jnp.bfloat16)

    def key_rows(index):
        return pl.ds(index * 2 * TILE, 2 * TILE)

    def fold(block, op):
        return op(block.reshape(2 * TILE // 8, 8, 2 * TILE), axis=0)

    def score_pair(pair, _):
        query_t = turned(pair_rows(q_all, pair))
        key_t[pair] = turned(pair_rows(k_all, pair))
        top = jnp.full((8, 2 * TILE), -3e38, jnp.float32)
        for chunk in range(pairs):
            scores = (
                jnp.dot(pair_rows(k_all, chunk), query_t, preferred_element_type=jnp.float32)
                * score_scale
            )
            scores = jnp.concatenate(
                [
                    scores[:TILE] + bias[pair, 2 * chunk : 2 * chunk + 1, :],
                    scores[TILE:] + bias[pair, 2 * chunk + 1 : 2 * chunk + 2, :],
                ],
                axis=0,
            )
            probs[pair, key_rows(chunk), :] = scores
            top = jnp.maximum(top, fold(scores, jnp.max))
        top = jnp.max(top, axis=0, keepdims=True)
        total = jnp.zeros((8, 2 * TILE), jnp.float32)
        for chunk in range(pairs):
            weights = jnp.exp(probs[pair, key_rows(chunk), :] - top)
            probs[pair, key_rows(chunk), :] = weights
            total = total + fold(weights, jnp.sum)
        inverse = 1.0 / jnp.sum(total, axis=0, keepdims=True)
        for chunk in range(pairs):
            probs[pair, key_rows(chunk), :] = probs[pair, key_rows(chunk), :] * inverse
        return 0

    lax.fori_loop(0, pairs, score_pair, 0)

    in_local(2).wait()
    for partner in partners:
        in_wait(2, *partner)

    def value_pair(pair, _):
        grad_pair = pair_rows(g_all, pair)
        for chunk in range(pairs):
            dv_sum[key_rows(chunk), :] += jnp.dot(
                probs[pair, key_rows(chunk), :].astype(jnp.bfloat16),
                grad_pair,
                preferred_element_type=jnp.float32,
            )
        return 0

    lax.fori_loop(0, pairs, value_pair, 0)
    dv_out[...] = dv_sum[...].astype(jnp.bfloat16).reshape(dv_out.shape)
    for partner in partners:
        out_copy(0, *partner).start()
    out_local(0).start()

    in_local(3).wait()
    for partner in partners:
        in_wait(3, *partner)

    def grad_pair_step(pair, _):
        query_pair = pair_rows(q_all, pair)
        grad_t = turned(pair_rows(g_all, pair))
        delta = jnp.zeros((8, 2 * TILE), jnp.float32)
        for chunk in range(pairs):
            product = jnp.dot(pair_rows(v_all, chunk), grad_t, preferred_element_type=jnp.float32)
            prob_grad[key_rows(chunk), :] = product
            rounded = probs[pair, key_rows(chunk), :].astype(jnp.bfloat16).astype(jnp.float32)
            delta = delta + fold(rounded * product, jnp.sum)
        delta = jnp.sum(delta, axis=0, keepdims=True)
        query_sum = jnp.zeros((DH, 2 * TILE), jnp.float32)
        for chunk in range(pairs):
            score_grad = (
                probs[pair, key_rows(chunk), :]
                * (prob_grad[key_rows(chunk), :] - delta)
                * score_scale
            ).astype(jnp.bfloat16)
            dk_sum[key_rows(chunk), :] += jnp.dot(
                score_grad, query_pair, preferred_element_type=jnp.float32
            )
            query_sum = query_sum + jnp.dot(
                key_t[chunk], score_grad, preferred_element_type=jnp.float32
            )
        dq_out[pl.ds(2 * pair, 2)] = query_sum.T.astype(jnp.bfloat16).reshape(2, TILE, DH)
        for side in range(2):
            there = 2 * pair + side

            @pl.when(there != me)
            def _():
                out_copy(1, lax.rem(there, seq_count), there // seq_count, there).start()

        return 0

    lax.fori_loop(0, pairs, grad_pair_step, 0)
    dk_out[...] = dk_sum[...].astype(jnp.bfloat16).reshape(dk_out.shape)
    for partner in partners:
        out_copy(2, *partner).start()
    out_local(1).start()
    out_local(2).start()

    for which in range(3):
        out_local(which).wait()
        for partner in partners:
            out_wait(which, *partner)


def settle_kernel(*refs):
    copies = [
        pltpu.make_async_copy(src, dst, refs[6].at[i])
        for i, (src, dst) in enumerate(zip(refs[:3], refs[3:6]))
    ]
    for copy in copies:
        copy.start()
    for copy in copies:
        copy.wait()


def settle(grads):
    anywhere = pl.BlockSpec(memory_space=pl.ANY)
    return pl.pallas_call(
        settle_kernel,
        out_shape=[pltpu.HBM(grad.shape, grad.dtype) for grad in grads],
        in_specs=[anywhere] * 3,
        out_specs=[anywhere] * 3,
        scratch_shapes=[pltpu.SemaphoreType.DMA((3,))],
    )(*[pltpu.with_memory_space_constraint(grad, pltpu.VMEM) for grad in grads])


def head_body(queries, keys, values, out_grad, tile_lists):
    seq_count = lax.axis_size("seq")
    tensor_count = lax.axis_size("tensor")
    tiles = seq_count * tensor_count
    pairs = tiles // 2
    shape = (TILE, HEADS * DH)
    blocks = [array.reshape(shape) for array in (queries, keys, values, out_grad)]
    anywhere = pl.BlockSpec(memory_space=pl.ANY)
    per_tile = pltpu.VMEM((tiles, TILE, DH), jnp.bfloat16)
    grads = pl.pallas_call(
        functools.partial(head_kernel, seq_count, tensor_count),
        out_shape=[pltpu.VMEM(shape, jnp.bfloat16)] * 3,
        in_specs=[anywhere] * 5,
        out_specs=[anywhere] * 3,
        scratch_shapes=[
            pltpu.VMEM((2, tiles, TILE, DH), jnp.bfloat16),
            per_tile,
            per_tile,
            pltpu.VMEM((tensor_count,) + tile_lists.shape, jnp.int32),
            pltpu.VMEM((pairs, tiles, 2 * TILE), jnp.float32),
            pltpu.VMEM((pairs, tiles * TILE, 2 * TILE), jnp.float32),
            pltpu.VMEM((tiles * TILE, 2 * TILE), jnp.float32),
            pltpu.VMEM((pairs, DH, 2 * TILE), jnp.bfloat16),
            pltpu.VMEM((tiles * TILE, DH), jnp.float32),
            pltpu.VMEM((tiles * TILE, DH), jnp.float32),
            per_tile,
            per_tile,
            per_tile,
            pltpu.VMEM((4,) + shape, jnp.bfloat16),
            pltpu.SemaphoreType.DMA((4, tiles)),
            pltpu.SemaphoreType.DMA((4, tiles)),
            pltpu.SemaphoreType.DMA((3, tiles)),
            pltpu.SemaphoreType.DMA((3, tiles)),
            pltpu.SemaphoreType.DMA((tensor_count,)),
            pltpu.SemaphoreType.DMA((tensor_count,)),
            pltpu.SemaphoreType.DMA((12,)),
        ],
        compiler_params=pltpu.CompilerParams(
            collective_id=0, has_side_effects=True, vmem_limit_bytes=60 * 1024 * 1024
        ),
    )(*blocks, tile_lists)
    return tuple(grad.reshape(queries.shape) for grad in settle(grads))


def body(queries, keys, values, out_grad, tile_lists):
    devices = lax.axis_size("seq") * lax.axis_size("tensor")
    one_head_one_tile = devices == HEADS and queries.shape[:2] == (1, TILE)
    if one_head_one_tile and queries.shape[2] == HEADS * DH:
        return head_body(queries, keys, values, out_grad, tile_lists)
    return regrouped_body(queries, keys, values, out_grad, tile_lists)


def solution(mesh):
    return jax.shard_map(
        body,
        mesh=mesh,
        in_specs=(
            P(("groups", "tensor"), "seq", None),
            P(("groups", "tensor"), "seq", None),
            P(("groups", "tensor"), "seq", None),
            P(("groups", "tensor"), "seq", None),
            P(("groups", "tensor"), None),
        ),
        out_specs=(
            P(("groups", "tensor"), "seq", None),
            P(("groups", "tensor"), "seq", None),
            P(("groups", "tensor"), "seq", None),
        ),
        check_vma=False,
    )
```

```python
import functools
import math

import jax
import jax.numpy as jnp
from jax import lax
from jax.experimental import pallas as pl
from jax.experimental.pallas import tpu as pltpu
from jax.sharding import PartitionSpec as P

HEADS = 16
DH = 128
TILE = 128
RADIUS = 8
WIN = 12


block_tiles = 4


def padded_2(block, sides, width):
    for axis, dim in sides:
        count = lax.axis_size(axis)
        forward = [(i, i + 1) for i in range(count - 1)]
        backward = [(target, source) for source, target in forward]
        low = lax.ppermute(
            lax.slice_in_dim(block, block.shape[dim] - width, None, axis=dim), axis, forward
        )
        high = lax.ppermute(lax.slice_in_dim(block, 0, width, axis=dim), axis, backward)
        block = jnp.concatenate([low, block, high], axis=dim)
    return block


def key_rims(key_rows, value_rows):
    joined = jnp.concatenate([key_rows, value_rows], 1)
    return padded_2(joined, (("tensor", 0),), RADIUS * TILE)


def finish_rims(grads_ext, segment, local_width):
    rim_rows = RADIUS * TILE
    outer_rows = jnp.concatenate([grads_ext[:rim_rows], grads_ext[-rim_rows:]], 0)
    arrived = padded_2(outer_rows, (("tensor", 0),), rim_rows)
    own_rows = grads_ext[rim_rows : rim_rows + segment]
    own_rows = own_rows.at[:rim_rows].add(arrived[:rim_rows])
    own_rows = own_rows.at[segment - rim_rows :].add(arrived[3 * rim_rows :])
    own_rows = own_rows.astype(jnp.bfloat16)
    return (own_rows[:, :local_width], own_rows[:, local_width:])


def regrouped_body(queries, keys, values, out_grad, tile_lists):
    span_rows = queries.shape[1]
    feature_count = queries.shape[2]
    seq_count = lax.axis_size("seq")
    heads_here = HEADS // seq_count
    local_width = heads_here * DH
    score_scale = 1.0 / math.sqrt(DH)
    query_tokens = queries.reshape(span_rows, feature_count)
    key_tokens = keys.reshape(span_rows, feature_count)
    value_tokens = values.reshape(span_rows, feature_count)
    grad_tokens = out_grad.reshape(span_rows, feature_count)
    query_rows, key_rows, value_rows, grad_rows = (
        lax.all_to_all(query_tokens, "seq", split_axis=1, concat_axis=0, tiled=True),
        lax.all_to_all(key_tokens, "seq", split_axis=1, concat_axis=0, tiled=True),
        lax.all_to_all(value_tokens, "seq", split_axis=1, concat_axis=0, tiled=True),
        lax.all_to_all(grad_tokens, "seq", split_axis=1, concat_axis=0, tiled=True),
    )
    padded = key_rims(key_rows, value_rows)
    segment = query_rows.shape[0]
    seg_tiles = segment // TILE
    ext_tiles = seg_tiles + 2 * RADIUS
    block_count = seg_tiles // block_tiles
    first_tile = lax.axis_index("tensor") * seg_tiles - RADIUS
    kv_tiles = padded.reshape(ext_tiles, TILE, 2 * local_width)
    query_blocks = query_rows.reshape(block_count, block_tiles, TILE, heads_here, DH)
    grad_blocks = grad_rows.reshape(block_count, block_tiles, TILE, heads_here, DH)
    list_blocks = tile_lists.reshape(block_count, block_tiles, WIN)

    def attend_block(totals, inputs):
        query_block, grad_block, tile_rows = inputs
        present = tile_rows >= 0
        local_tile = jnp.clip(tile_rows - first_tile, 0, ext_tiles - 1)
        picked = kv_tiles[local_tile].reshape(block_tiles, WIN * TILE, 2, heads_here, DH)
        key_sel = picked[:, :, 0]
        value_sel = picked[:, :, 1]
        scores = (
            jnp.einsum("gthd,gkhd->ghtk", query_block, key_sel, preferred_element_type=jnp.float32)
            * score_scale
        )
        live_keys = jnp.repeat(present, TILE, axis=1)
        scores = jnp.where(live_keys[:, None, None, :], scores, -1e30)
        row_max = jnp.max(scores, axis=3, keepdims=True)
        weights = jnp.exp(scores - row_max)
        weights = weights / jnp.sum(weights, axis=3, keepdims=True)
        weights_b = weights.astype(jnp.bfloat16)
        recomputed = jnp.einsum(
            "ghtk,gkhd->gthd", weights_b, value_sel, preferred_element_type=jnp.float32
        )
        delta = jnp.sum(grad_block.astype(jnp.float32) * recomputed, axis=3)
        prob_grad = jnp.einsum(
            "gthd,gkhd->ghtk", grad_block, value_sel, preferred_element_type=jnp.float32
        )
        score_grad = (
            weights * (prob_grad - jnp.transpose(delta, (0, 2, 1))[..., None]) * score_scale
        ).astype(jnp.bfloat16)
        query_part = jnp.einsum(
            "ghtk,gkhd->gthd", score_grad, key_sel, preferred_element_type=jnp.float32
        ).astype(jnp.bfloat16)
        key_part = jnp.einsum(
            "ghtk,gthd->gkhd", score_grad, query_block, preferred_element_type=jnp.float32
        )
        value_part = jnp.einsum(
            "ghtk,gthd->gkhd", weights_b, grad_block, preferred_element_type=jnp.float32
        )
        key_terms = jnp.concatenate([key_part, value_part], 2).reshape(
            block_tiles, WIN, TILE, 2 * local_width
        )
        totals = totals.at[local_tile].add(key_terms)
        return (totals, query_part)

    initial = jnp.zeros((ext_tiles, TILE, 2 * local_width), jnp.float32)
    grads_ext, query_parts = lax.scan(
        attend_block, initial, (query_blocks, grad_blocks, list_blocks)
    )
    query_grad = query_parts.reshape(segment, local_width)
    grads_ext = grads_ext.reshape(ext_tiles * TILE, 2 * local_width)
    query_back = lax.all_to_all(query_grad, "seq", split_axis=0, concat_axis=1, tiled=True)
    key_grad, value_grad = finish_rims(grads_ext, segment, local_width)
    key_back, value_back = (
        lax.all_to_all(key_grad, "seq", split_axis=0, concat_axis=1, tiled=True),
        lax.all_to_all(value_grad, "seq", split_axis=0, concat_axis=1, tiled=True),
    )
    out_shape = queries.shape
    return (
        query_back.reshape(out_shape),
        key_back.reshape(out_shape),
        value_back.reshape(out_shape),
    )


def partner_order(seq_count, tensor_count):
    order = []
    for step in range(seq_count):
        reach = (seq_count // 2 + ((step + 1) // 2) * (1 - 2 * (step % 2))) % seq_count
        for turn in range(tensor_count):
            if reach or turn:
                order.append((reach, turn))
    return order


def head_kernel(
    seq_count,
    tensor_count,
    q_hbm,
    k_hbm,
    v_hbm,
    g_hbm,
    lists_hbm,
    dq_hbm,
    dk_hbm,
    dv_hbm,
    qk_all,
    v_all,
    g_all,
    lists_all,
    bias,
    probs,
    prob_grad,
    key_t,
    dv_sum,
    dk_sum,
    dq_out,
    dk_out,
    dv_out,
    staged,
    in_send,
    in_recv,
    out_send,
    out_recv,
    list_send,
    list_recv,
    local_sem,
):
    seq_here = lax.axis_index("seq")
    tensor_here = lax.axis_index("tensor")
    me = tensor_here * seq_count + seq_here
    tiles = seq_count * tensor_count
    pairs = tiles // 2
    score_scale = 1.0 / math.sqrt(DH)
    partners = []
    for reach, turn in partner_order(seq_count, tensor_count):
        seq_there = lax.rem(seq_here + reach, seq_count)
        tensor_there = lax.rem(tensor_here + turn, tensor_count)
        partners.append((seq_there, tensor_there, tensor_there * seq_count + seq_there))

    def columns(index):
        return pl.ds(pl.multiple_of(index * DH, DH), DH)

    def remote(src, dst, send, recv, seq_there, tensor_there):
        return pltpu.make_async_remote_copy(
            src_ref=src,
            dst_ref=dst,
            send_sem=send,
            recv_sem=recv,
            device_id={"seq": seq_there, "tensor": tensor_there},
            device_id_type=pl.DeviceIdType.MESH,
        )

    staging = [
        pltpu.make_async_copy(src, staged.at[which], local_sem.at[8 + which])
        for which, src in enumerate((q_hbm, k_hbm, g_hbm, v_hbm))
    ]
    q_all, k_all = qk_all.at[0], qk_all.at[1]
    incoming = {
        0: (lambda cols: staged.at[pl.ds(0, 2), :, cols], lambda slot: qk_all.at[:, slot]),
        2: (lambda cols: staged.at[2, :, cols], lambda slot: g_all.at[slot]),
        3: (lambda cols: staged.at[3, :, cols], lambda slot: v_all.at[slot]),
    }
    outgoing = ((dv_out, dv_hbm), (dq_out, dq_hbm), (dk_out, dk_hbm))

    def in_copy(which, seq_there, tensor_there, there):
        src, dst = incoming[which]
        return remote(
            src(columns(there)),
            dst(me),
            in_send.at[which, there],
            in_recv.at[which, me],
            seq_there,
            tensor_there,
        )

    def in_wait(which, seq_there, tensor_there, there):
        src, dst = incoming[which]
        remote(
            src(columns(there)),
            dst(there),
            in_send.at[which, there],
            in_recv.at[which, there],
            seq_there,
            tensor_there,
        ).wait()

    def in_local(which):
        src, dst = incoming[which]
        return pltpu.make_async_copy(src(columns(me)), dst(me), local_sem.at[which])

    def out_copy(which, seq_there, tensor_there, there):
        src, dst = outgoing[which]
        return remote(
            src.at[there],
            dst.at[:, columns(me)],
            out_send.at[which, there],
            out_recv.at[which, me],
            seq_there,
            tensor_there,
        )

    def out_wait(which, seq_there, tensor_there, there):
        src, dst = outgoing[which]
        remote(
            src.at[there],
            dst.at[:, columns(there)],
            out_send.at[which, there],
            out_recv.at[which, there],
            seq_there,
            tensor_there,
        ).wait()

    def out_local(which):
        src, dst = outgoing[which]
        return pltpu.make_async_copy(src.at[me], dst.at[:, columns(me)], local_sem.at[4 + which])

    for copy in staging:
        copy.start()
    own_list = pltpu.make_async_copy(lists_hbm, lists_all.at[tensor_here], local_sem.at[7])
    own_list.start()

    barrier = pltpu.get_barrier_semaphore()
    for seq_there, tensor_there, _ in partners:
        pl.semaphore_signal(
            barrier,
            inc=1,
            device_id={"seq": seq_there, "tensor": tensor_there},
            device_id_type=pl.DeviceIdType.MESH,
        )
    pl.semaphore_wait(barrier, len(partners))

    def list_copy(turn, slot):
        return remote(
            lists_hbm,
            lists_all.at[slot],
            list_send.at[turn],
            list_recv.at[slot],
            seq_here,
            lax.rem(tensor_here + turn, tensor_count),
        )

    for turn in range(1, tensor_count):
        list_copy(turn, tensor_here).start()
    for group in ((0, 1), (2,), (3,)):
        for which in group:
            staging[which].wait()
        in_local(group[0]).start()
        for partner in partners:
            in_copy(group[0], *partner).start()

    own_list.wait()
    for turn in range(1, tensor_count):
        list_copy(turn, lax.rem(tensor_here + turn, tensor_count)).wait()
    tile_ids = lax.broadcasted_iota(jnp.int32, (tiles, TILE), 0)
    for tile in range(tiles):
        row = lists_all[tile // seq_count, tile % seq_count : tile % seq_count + 1, :]
        miss = jnp.full((tiles, TILE), -1e30, jnp.float32)
        for entry in range(WIN):
            miss = jnp.where(row[:, entry : entry + 1] == tile_ids, 0.0, miss)
        half = (tile % 2) * TILE
        bias[tile // 2, :, half : half + TILE] = miss

    dv_sum[...] = jnp.zeros_like(dv_sum)
    dk_sum[...] = jnp.zeros_like(dk_sum)

    in_local(0).wait()
    for partner in partners:
        in_wait(0, *partner)

    def pair_rows(ref, index):
        return ref[pl.ds(2 * index, 2)].reshape(2 * TILE, DH)

    def turned(block):
        return block.astype(jnp.float32).T.astype(jnp.bfloat16)

    def key_rows(index):
        return pl.ds(index * 2 * TILE, 2 * TILE)

    def fold(block, op):
        return op(block.reshape(2 * TILE // 8, 8, 2 * TILE), axis=0)

    def score_pair(pair, _):
        query_t = turned(pair_rows(q_all, pair))
        key_t[pair] = turned(pair_rows(k_all, pair))
        top = jnp.full((8, 2 * TILE), -3e38, jnp.float32)
        for chunk in range(pairs):
            scores = (
                jnp.dot(pair_rows(k_all, chunk), query_t, preferred_element_type=jnp.float32)
                * score_scale
            )
            scores = jnp.concatenate(
                [
                    scores[:TILE] + bias[pair, 2 * chunk : 2 * chunk + 1, :],
                    scores[TILE:] + bias[pair, 2 * chunk + 1 : 2 * chunk + 2, :],
                ],
                axis=0,
            )
            probs[pair, key_rows(chunk), :] = scores
            top = jnp.maximum(top, fold(scores, jnp.max))
        top = jnp.max(top, axis=0, keepdims=True)
        total = jnp.zeros((8, 2 * TILE), jnp.float32)
        for chunk in range(pairs):
            weights = jnp.exp(probs[pair, key_rows(chunk), :] - top)
            probs[pair, key_rows(chunk), :] = weights
            total = total + fold(weights, jnp.sum)
        inverse = 1.0 / jnp.sum(total, axis=0, keepdims=True)
        for chunk in range(pairs):
            probs[pair, key_rows(chunk), :] = probs[pair, key_rows(chunk), :] * inverse
        return 0

    lax.fori_loop(0, pairs, score_pair, 0)

    in_local(2).wait()
    for partner in partners:
        in_wait(2, *partner)

    def value_pair(pair, _):
        grad_pair = pair_rows(g_all, pair)
        for chunk in range(pairs):
            dv_sum[key_rows(chunk), :] += jnp.dot(
                probs[pair, key_rows(chunk), :].astype(jnp.bfloat16),
                grad_pair,
                preferred_element_type=jnp.float32,
            )
        return 0

    lax.fori_loop(0, pairs, value_pair, 0)
    dv_out[...] = dv_sum[...].astype(jnp.bfloat16).reshape(dv_out.shape)
    for partner in partners:
        out_copy(0, *partner).start()
    out_local(0).start()

    in_local(3).wait()
    for partner in partners:
        in_wait(3, *partner)

    def grad_pair_step(pair, _):
        query_pair = pair_rows(q_all, pair)
        grad_t = turned(pair_rows(g_all, pair))
        delta = jnp.zeros((8, 2 * TILE), jnp.float32)
        for chunk in range(pairs):
            product = jnp.dot(pair_rows(v_all, chunk), grad_t, preferred_element_type=jnp.float32)
            prob_grad[key_rows(chunk), :] = product
            rounded = probs[pair, key_rows(chunk), :].astype(jnp.bfloat16).astype(jnp.float32)
            delta = delta + fold(rounded * product, jnp.sum)
        delta = jnp.sum(delta, axis=0, keepdims=True)
        query_sum = jnp.zeros((DH, 2 * TILE), jnp.float32)
        for chunk in range(pairs):
            score_grad = (
                probs[pair, key_rows(chunk), :]
                * (prob_grad[key_rows(chunk), :] - delta)
                * score_scale
            ).astype(jnp.bfloat16)
            dk_sum[key_rows(chunk), :] += jnp.dot(
                score_grad, query_pair, preferred_element_type=jnp.float32
            )
            query_sum = query_sum + jnp.dot(
                key_t[chunk], score_grad, preferred_element_type=jnp.float32
            )
        dq_out[pl.ds(2 * pair, 2)] = query_sum.T.astype(jnp.bfloat16).reshape(2, TILE, DH)
        for side in range(2):
            there = 2 * pair + side

            @pl.when(there != me)
            def _():
                out_copy(1, lax.rem(there, seq_count), there // seq_count, there).start()

        return 0

    lax.fori_loop(0, pairs, grad_pair_step, 0)
    dk_out[...] = dk_sum[...].astype(jnp.bfloat16).reshape(dk_out.shape)
    for partner in partners[1::2] + partners[::2]:
        out_copy(2, *partner).start()
    out_local(1).start()
    out_local(2).start()

    for which in range(3):
        out_local(which).wait()
        for partner in partners:
            out_wait(which, *partner)


def settle_kernel(*refs):
    copies = [
        pltpu.make_async_copy(src, dst, refs[6].at[i])
        for i, (src, dst) in enumerate(zip(refs[:3], refs[3:6]))
    ]
    for copy in copies:
        copy.start()
    for copy in copies:
        copy.wait()


def settle(grads):
    anywhere = pl.BlockSpec(memory_space=pl.ANY)
    return pl.pallas_call(
        settle_kernel,
        out_shape=[pltpu.HBM(grad.shape, grad.dtype) for grad in grads],
        in_specs=[anywhere] * 3,
        out_specs=[anywhere] * 3,
        scratch_shapes=[pltpu.SemaphoreType.DMA((3,))],
    )(*[pltpu.with_memory_space_constraint(grad, pltpu.VMEM) for grad in grads])


def head_body(queries, keys, values, out_grad, tile_lists):
    seq_count = lax.axis_size("seq")
    tensor_count = lax.axis_size("tensor")
    tiles = seq_count * tensor_count
    pairs = tiles // 2
    shape = (TILE, HEADS * DH)
    blocks = [array.reshape(shape) for array in (queries, keys, values, out_grad)]
    anywhere = pl.BlockSpec(memory_space=pl.ANY)
    per_tile = pltpu.VMEM((tiles, TILE, DH), jnp.bfloat16)
    grads = pl.pallas_call(
        functools.partial(head_kernel, seq_count, tensor_count),
        out_shape=[pltpu.VMEM(shape, jnp.bfloat16)] * 3,
        in_specs=[anywhere] * 5,
        out_specs=[anywhere] * 3,
        scratch_shapes=[
            pltpu.VMEM((2, tiles, TILE, DH), jnp.bfloat16),
            per_tile,
            per_tile,
            pltpu.VMEM((tensor_count,) + tile_lists.shape, jnp.int32),
            pltpu.VMEM((pairs, tiles, 2 * TILE), jnp.float32),
            pltpu.VMEM((pairs, tiles * TILE, 2 * TILE), jnp.float32),
            pltpu.VMEM((tiles * TILE, 2 * TILE), jnp.float32),
            pltpu.VMEM((pairs, DH, 2 * TILE), jnp.bfloat16),
            pltpu.VMEM((tiles * TILE, DH), jnp.float32),
            pltpu.VMEM((tiles * TILE, DH), jnp.float32),
            per_tile,
            per_tile,
            per_tile,
            pltpu.VMEM((4,) + shape, jnp.bfloat16),
            pltpu.SemaphoreType.DMA((4, tiles)),
            pltpu.SemaphoreType.DMA((4, tiles)),
            pltpu.SemaphoreType.DMA((3, tiles)),
            pltpu.SemaphoreType.DMA((3, tiles)),
            pltpu.SemaphoreType.DMA((tensor_count,)),
            pltpu.SemaphoreType.DMA((tensor_count,)),
            pltpu.SemaphoreType.DMA((12,)),
        ],
        compiler_params=pltpu.CompilerParams(
            collective_id=0, has_side_effects=True, vmem_limit_bytes=60 * 1024 * 1024
        ),
    )(*blocks, tile_lists)
    return tuple(grad.reshape(queries.shape) for grad in settle(grads))


def body(queries, keys, values, out_grad, tile_lists):
    devices = lax.axis_size("seq") * lax.axis_size("tensor")
    one_head_one_tile = devices == HEADS and queries.shape[:2] == (1, TILE)
    if one_head_one_tile and queries.shape[2] == HEADS * DH:
        return head_body(queries, keys, values, out_grad, tile_lists)
    return regrouped_body(queries, keys, values, out_grad, tile_lists)


def solution(mesh):
    return jax.shard_map(
        body,
        mesh=mesh,
        in_specs=(
            P(("groups", "tensor"), "seq", None),
            P(("groups", "tensor"), "seq", None),
            P(("groups", "tensor"), "seq", None),
            P(("groups", "tensor"), "seq", None),
            P(("groups", "tensor"), None),
        ),
        out_specs=(
            P(("groups", "tensor"), "seq", None),
            P(("groups", "tensor"), "seq", None),
            P(("groups", "tensor"), "seq", None),
        ),
        check_vma=False,
    )
```
